512 devices in a mesh: seq: 64 (over z, x), head: 8 (over y, core).
Axes of the slice: x: 4, y: 4, z: 16, core: 2. Of those that a mesh axis runs over, the one named last changes fastest.
Arguments:
- activations: bfloat16 [32768, 2048], P('seq', 'head'), may hold values from -6 to 6
- w_proj: bfloat16 [3, 2048, 2048], P(None, None, 'head'), may hold values from -0.125 to 0.125
- level_weight: float32 [32768, 16, 16], P('seq', 'head'), may hold values from 0.25 to 4
- grad_out: bfloat16 [32768, 2048], P('seq', 'head'), may hold values from -6 to 6
Outputs:
- attn_output: bfloat16 [32768, 2048], P('seq', 'head')
- grad_query: bfloat16 [32768, 2048], P('seq', 'head')
- grad_key: bfloat16 [32768, 2048], P('seq', 'head')
- grad_value: bfloat16 [32768, 2048], P('seq', 'head')
The draws below stay inside these ranges and needn't reach their ends.
All inputs are finite; a program needn't handle non-finite values.
Results may differ from the reference program's by a relative error of at most 0.0085.
Values may be sent and summed in bfloat16 or wider, within the bound.
No kernel may reach another device: no remote copies, remote signals or barrier semaphores. Data moves between devices by JAX's collectives and lax.ppermute only.
A program may use at most 64 MiB of HBM per device.

```python
import math
import jax
import jax.numpy as jnp
from jax import lax

D = 2048
HEADS = 16
HEAD_DIM = 128
TOK_DEV = 512
TOKENS = 32768
LEVELS = 16
N_SEQ = 64


def steps_of(stream_key, extent, shards, least, top_value):
    factor_of = 1.0
    for position, shards_of in shards:
        steps = jax.random.uniform(jax.random.fold_in(jax.random.fold_in(stream_key, 6), position), (shards_of,), jnp.float32, least / len(shards), top_value / len(shards))
        factor_of = factor_of * jnp.repeat(jnp.exp(steps), extent[position] // shards_of).reshape((-1,) + (1,) * (len(extent) - 1 - position))
    return factor_of


def bell_draw(key, dims, scale, bound, pieces=(), held_as=jnp.bfloat16):
    loudness = steps_of(key, dims, pieces, -0.22, 0.18) if pieces else 1.0
    values = jax.random.normal(key, dims, jnp.float32) * scale * loudness
    return jnp.minimum(jnp.maximum(values, -bound), bound).astype(held_as)


def setup_inputs(seed: int = 0) -> dict:
    seeds = jax.random.split(jax.random.key(seed), 5)
    activations = bell_draw(seeds[0], (TOKENS, D), 1.0, 6.0, ((0, 64), (1, 8)))
    w_proj = bell_draw(seeds[1], (3, D, D), D ** -0.5, 0.125, ((2, 8),))
    level_weight = jnp.clip(jnp.exp(math.log(4.0) - 2.7725887 * jax.random.uniform(seeds[2], (TOKENS, HEADS, LEVELS), jnp.float32) ** steps_of(seeds[2], (TOKENS, HEADS, LEVELS), ((0, 64), (1, 8)), -0.2, 0.2)), 0.25, 4.0)
    grad_out = bell_draw(seeds[3], (TOKENS, D), 1.0, 6.0, ((0, 64), (1, 8)))
    return dict(activations=activations, w_proj=w_proj, level_weight=level_weight, grad_out=grad_out)


def bit_length_of(numbers, width):
    total = jnp.zeros_like(numbers)
    for shift_by in range(width):
        total = total + (jnp.right_shift(numbers, shift_by) > 0).astype(jnp.int32)
    return total


def level_factors(count):
    index_list = jnp.arange(count, dtype=jnp.int32)
    return jnp.exp2(-0.5 * (jnp.maximum(index_list, 1) - 1).astype(jnp.float32))


def reference(activations, w_proj, level_weight, grad_out):
    scale = HEAD_DIM ** -0.5
    block_len = TOK_DEV
    block_bits = TOK_DEV.bit_length() - 1
    seq_bits = N_SEQ.bit_length() - 1
    blocks = N_SEQ
    highest = lax.Precision.HIGHEST

    def split_heads(matrix):
        return matrix.reshape(blocks, block_len, HEADS, HEAD_DIM).transpose(2, 0, 1, 3)

    query_all = split_heads(jnp.dot(activations, w_proj[0], preferred_element_type=jnp.float32).astype(jnp.bfloat16))
    key_all = split_heads(jnp.dot(activations, w_proj[1], preferred_element_type=jnp.float32).astype(jnp.bfloat16))
    value_all = split_heads(jnp.dot(activations, w_proj[2], preferred_element_type=jnp.float32).astype(jnp.bfloat16))
    cotan_all = split_heads(grad_out)
    weight = level_weight * level_factors(LEVELS)
    weight = weight.reshape(blocks, block_len, HEADS, LEVELS).transpose(2, 0, 1, 3)

    local_pos = jnp.arange(block_len, dtype=jnp.int32)
    local_level = bit_length_of(jnp.bitwise_xor(local_pos[:, None], local_pos[None, :]), block_bits)
    causal = local_pos[None, :] <= local_pos[:, None]
    block_ids = jnp.arange(blocks, dtype=jnp.int32)
    differ = jnp.bitwise_xor(block_ids[:, None], block_ids[None, :])
    earlier = block_ids[None, :] < block_ids[:, None]
    select = jnp.stack([earlier & (jnp.right_shift(differ, bit_index) == 1) for bit_index in range(seq_bits)], 1).astype(jnp.float32)

    def one_head(operands):
        query_rows, key_rows, value_rows, cotangent, head_weight = operands
        query_f = query_rows.astype(jnp.float32)
        key_f = key_rows.astype(jnp.float32)
        value_f = value_rows.astype(jnp.float32)
        cotan_f = cotangent.astype(jnp.float32)
        mask_weight = jnp.zeros((blocks, block_len, block_len), jnp.float32)
        for level_ix in range(block_bits + 1):
            chosen = (local_level == level_ix) & causal
            mask_weight = mask_weight + jnp.where(chosen[None], head_weight[:, :, level_ix][:, :, None], 0.0)
        scores = jnp.einsum("ntd,nsd->nts", query_f, key_f) * scale
        attn = (scores * mask_weight).astype(jnp.bfloat16).astype(jnp.float32)
        out_inner = jnp.einsum("nts,nsd->ntd", attn, value_f)
        back = jnp.einsum("ntd,nsd->nts", cotan_f, value_f)
        grads = (back * mask_weight * scale).astype(jnp.bfloat16).astype(jnp.float32)
        dq_inner = jnp.einsum("nts,nsd->ntd", grads, key_f)
        dk_inner = jnp.einsum("nts,ntd->nsd", grads, query_f)
        dv_inner = jnp.einsum("nts,ntd->nsd", attn, cotan_f)
        cross = head_weight[:, :, block_bits + 1:]
        states = jnp.einsum("nsx,nsy->nxy", key_f, value_f)
        prefix = jnp.einsum("dje,exy->djxy", select, states, precision=highest).astype(jnp.bfloat16).astype(jnp.float32)
        reads = jnp.einsum("ntx,njxy->ntjy", query_f, prefix)
        out_cross = scale * jnp.sum(cross[..., None] * reads, 2)
        reads_back = jnp.einsum("nty,njxy->ntjx", cotan_f, prefix)
        dq_cross = scale * jnp.sum(cross[..., None] * reads_back, 2)
        weighted = cross[:, :, :, None] * query_f[:, :, None, :]
        level_grads = jnp.einsum("ntjx,nty->njxy", weighted, cotan_f, precision=highest)
        suffix = jnp.einsum("dje,djxy->ejxy", select, level_grads, precision=highest).astype(jnp.bfloat16).astype(jnp.float32)
        dk_cross = scale * jnp.einsum("nsy,njxy->nsx", value_f, suffix)
        dv_cross = scale * jnp.einsum("nsx,njxy->nsy", key_f, suffix)
        return (out_inner + out_cross, dq_inner + dq_cross, dk_inner + dk_cross, dv_inner + dv_cross)

    results = lax.map(one_head, (query_all, key_all, value_all, cotan_all, weight))

    def merge_heads(array):
        return array.transpose(1, 2, 0, 3).reshape(TOKENS, D).astype(jnp.bfloat16)

    return (merge_heads(results[0]), merge_heads(results[1]), merge_heads(results[2]), merge_heads(results[3]))
```

```python
import functools

import jax
import jax.numpy as jnp
from jax import lax
from jax.experimental import pallas as pl
from jax.experimental.pallas import tpu as pltpu
from jax.sharding import Mesh, PartitionSpec as P

T = 512
D = 128
H = 2
NX = 4
NZ = 16
NY = 4
Q = D // NX
DIRECT = 5 * H * Q
MSG = DIRECT + H * D
F32 = jnp.float32
BF16 = jnp.bfloat16


def dot(a, b):
    return jnp.dot(a, b, preferred_element_type=F32)


def dot_nt(a, b):
    return lax.dot_general(a, b, (((1,), (1,)), ((), ())), preferred_element_type=F32)


def flipped(a):
    return a.astype(F32).T


def level_scale(level):
    return 2.0 ** (-(max(level, 1) - 1) / 2) * D**-0.5


def project_kernel(pos, xa, xb, w, lw, g, q_out, k_out, v_out, msg, x_all):
    core, x = pos[0], pos[1]
    for y in range(NY):
        at_a = pl.multiple_of((2 * y + core) * 256, 256)
        at_b = pl.multiple_of((2 * y + 1 - core) * 256, 256)
        x_all[:, pl.ds(at_a, 256)] = xa[y]
        x_all[:, pl.ds(at_b, 256)] = xb[y]
    q = dot(x_all[...], w[0]).astype(BF16)
    k = dot(x_all[...], w[1]).astype(BF16)
    v = dot(x_all[...], w[2]).astype(BF16)
    q_out[...] = q
    k_out[...] = k
    v_out[...] = v
    for h in range(H):
        cols = slice(h * D, (h + 1) * D)
        q_t = flipped(q[:, cols])
        g_h = g[:, cols]
        mats = [dot(flipped(k[:, cols]).astype(BF16), v[:, cols])]
        for j in range(6):
            row = lw[h, 10 + j : 11 + j, :] * level_scale(10 + j)
            mats.append(dot((q_t * row).astype(BF16), g_h))
        state, r0, r1 = mats[0], mats[1], mats[2]
        for to in range(NX):
            direct = jnp.where(to > x, state, jnp.where((x ^ to) >= 2, r1, r0))
            at = DIRECT + h * D
            msg[to, at : at + D, :] = direct.astype(BF16)
            for m, mat in enumerate([state] + mats[3:]):
                at = (m * H + h) * Q
                msg[to, at : at + Q, :] = mat[to * Q : (to + 1) * Q].astype(BF16)


def spread_kernel(pos, recv, out, mats):
    z = pos[2]
    total = recv[0, :DIRECT, :].astype(F32)
    for src in range(1, NX):
        total = total + recv[src, :DIRECT, :].astype(F32)
    mats[...] = total.astype(BF16).reshape(5, H * Q, D)
    for to in range(NZ):
        d = z ^ to
        top = (d >= 2).astype(jnp.int32) + (d >= 4).astype(jnp.int32) + (d >= 8).astype(jnp.int32)
        out[to] = mats[jnp.where(to > z, 0, 1 + top)]


def collect_kernel(pos, recv, out):
    z = pos[2]
    for j in range(4):
        first = lax.shift_left(lax.shift_right_logical(z, j) ^ 1, j)
        total = recv[first].astype(F32)
        for i in range(1, 2**j):
            total = total + recv[first + i].astype(F32)
        total = total.astype(BF16)
        for to in range(NX):
            out[to, j * H * Q : (j + 1) * H * Q, :] = total


def attend_kernel(q_in, k_in, v_in, g_in, lw, out_t, dq_t, dk, dv, a_t, b_t):
    n = T // D
    s_at = lax.broadcasted_iota(jnp.int32, (D, D), 0)
    t_at = lax.broadcasted_iota(jnp.int32, (D, D), 1)
    differ = s_at ^ t_at
    for h in range(H):
        cols = slice(h * D, (h + 1) * D)
        q, k, v, g = q_in[:, cols], k_in[:, cols], v_in[:, cols], g_in[:, cols]
        q_t, k_t, v_t, g_t = (flipped(a).astype(BF16) for a in (q, k, v, g))
        rows = [lw[h, l : l + 1, :] * level_scale(l) for l in range(10)]
        for si in range(n):
            s = slice(si * D, (si + 1) * D)
            scores = dot(k[s], q_t[:, si * D :])
            back = dot(v[s], g_t[:, si * D :])
            for ti in range(si, n):
                t = slice(ti * D, (ti + 1) * D)
                part = slice((ti - si) * D, (ti - si + 1) * D)
                if ti == si:
                    mask = jnp.broadcast_to(rows[0][:, t], (D, D))
                    for l in range(1, 8):
                        mask = jnp.where(differ >= 2 ** (l - 1), rows[l][:, t], mask)
                    mask = jnp.where(t_at >= s_at, mask, 0.0)
                else:
                    mask = rows[8 if ti ^ si == 1 else 9][:, t]
                a_t[s, t] = (scores[:, part] * mask).astype(BF16)
                b_t[s, t] = (back[:, part] * mask).astype(BF16)
            dv[s, cols] = dot(a_t[s, si * D :], g[si * D :])
            dk[s, cols] = dot(b_t[s, si * D :], q[si * D :])
        for ti in range(n):
            t = slice(ti * D, (ti + 1) * D)
            seen = (ti + 1) * D
            out_t[h, :, t] = dot(v_t[:, :seen], a_t[:seen, t])
            dq_t[h, :, t] = dot(k_t[:, :seen], b_t[:seen, t])


def finish_kernel(pos, q_in, k_in, v_in, g_in, lw, recv_a, recv_c, out_p, dq_p, dk_p, dv_p, out, dq, dk, dv):
    x, n = pos[1], pos[3]
    for h in range(H):
        cols = slice(h * D, (h + 1) * D)
        at = DIRECT + h * D
        near = [recv_a[x ^ i, at : at + D, :].astype(F32) for i in (1, 2, 3)]
        slots = [near[0], near[1] + near[2]]
        for j in range(4):
            at = (j * H + h) * Q
            slots.append(
                jnp.concatenate([recv_c[src, at : at + Q, :].astype(F32) for src in range(NX)], 0)
            )
        q_t, g_t = flipped(q_in[:, cols]), flipped(g_in[:, cols])
        total_o, total_q = out_p[h], dq_p[h]
        later = jnp.zeros((D, D), F32)
        for j in range(6):
            flag = (lax.shift_right_logical(n, j) & 1).astype(F32)
            row = lw[h, 10 + j : 11 + j, :] * (level_scale(10 + j) * flag)
            total_o = total_o + dot(slots[j].T.astype(BF16), (q_t * row).astype(BF16))
            total_q = total_q + dot(slots[j].astype(BF16), (g_t * row).astype(BF16))
            later = later + slots[j] * (1.0 - flag)
        later = later.astype(BF16)
        out[:, cols] = total_o.T.astype(BF16)
        dq[:, cols] = total_q.T.astype(BF16)
        dk[:, cols] = (dk_p[:, cols] + dot_nt(v_in[:, cols], later)).astype(BF16)
        dv[:, cols] = (dv_p[:, cols] + dot(k_in[:, cols], later)).astype(BF16)


SMEM = pl.BlockSpec(memory_space=pltpu.SMEM)
VMEM = pl.BlockSpec(memory_space=pltpu.VMEM)


def call(kernel, pos, args, outs, scratch=()):
    shapes = tuple(jax.ShapeDtypeStruct(s, d) for s, d in outs)
    head = () if pos is None else (pos,)
    return pl.pallas_call(
        kernel,
        out_shape=shapes,
        in_specs=[SMEM] * len(head) + [VMEM] * len(args),
        out_specs=tuple(VMEM for _ in shapes),
        scratch_shapes=list(scratch),
        compiler_params=pltpu.CompilerParams(vmem_limit_bytes=40 * 2**20),
    )(*head, *args)


def swap(value, axis):
    return lax.all_to_all(value, axis, 0, 0, tiled=True)


def on_device(activations, w_proj, level_weight, g):
    z, x, core = lax.axis_index("z"), lax.axis_index("x"), lax.axis_index("core")
    pos = jnp.stack([core, x, z, z * NX + x]).astype(jnp.int32)
    lw = jnp.transpose(level_weight, (1, 2, 0))
    xa = swap(jnp.broadcast_to(activations[None], (NY, *activations.shape)), "y")
    xb = lax.ppermute(xa, "core", [(0, 1), (1, 0)])
    tokens = ((T, H * D), BF16)
    q, k, v, msg = call(
        project_kernel,
        pos,
        (xa, xb, w_proj, lw, g),
        (tokens, tokens, tokens, ((NX, MSG, D), BF16)),
        [pltpu.VMEM((T, 2048), BF16)],
    )
    recv_a = swap(msg, "x")
    (far,) = call(
        spread_kernel, pos, (recv_a,), (((NZ, H * Q, D), BF16),), [pltpu.VMEM((5, H * Q, D), BF16)]
    )
    recv_b = swap(far, "z")
    (back,) = call(collect_kernel, pos, (recv_b,), (((NX, 4 * H * Q, D), BF16),))
    recv_c = swap(back, "x")
    flat, tall = ((T, H * D), F32), ((H, D, T), F32)
    parts = call(
        attend_kernel,
        None,
        (q, k, v, g, lw),
        (tall, tall, flat, flat),
        [pltpu.VMEM((T, T), BF16), pltpu.VMEM((T, T), BF16)],
    )
    return call(
        finish_kernel, pos, (q, k, v, g, lw, recv_a, recv_c, *parts), (tokens,) * 4
    )


def solution(mesh):
    fine = Mesh(mesh.devices.reshape(NZ, NX, NY, 2), ("z", "x", "y", "core"))
    rows, cols = ("z", "x"), ("y", "core")
    in_specs = (P(rows, cols), P(None, None, cols), P(rows, cols, None), P(rows, cols))
    return jax.shard_map(
        on_device, mesh=fine, in_specs=in_specs, out_specs=(P(rows, cols),) * 4, check_vma=False
    )
```

```python
import jax
import jax.numpy as jnp
from jax import lax
from jax.experimental import pallas as pl
from jax.experimental.pallas import tpu as pltpu
from jax.sharding import Mesh, PartitionSpec as P

T = 512
D = 128
H = 2
NX = 4
NL = 2
NG = NX * NL
NZ = 8
NY = 4
Q = D // NG
HQ = H * Q
F32 = jnp.float32
BF16 = jnp.bfloat16


def dot(a, b):
    return jnp.dot(a, b, preferred_element_type=F32)


def dot_nt(a, b):
    return lax.dot_general(a, b, (((1,), (1,)), ((), ())), preferred_element_type=F32)


def flipped(a):
    return a.astype(F32).T


def level_scale(level):
    return 2.0 ** (-(max(level, 1) - 1) / 2) * D**-0.5


def half_kernel(pos, xa, w, lw, g, part, w_rest, g6, w_mine, sems):
    core = pos[0]
    copies = [
        pltpu.make_async_copy(w.at[c, :, side], to.at[c], sems.at[i, c])
        for i, (side, to) in enumerate(((core, w_mine), (1 - core, w_rest)))
        for c in range(3)
    ]
    for copy in copies:
        copy.start()
    for h in range(H):
        g_t = flipped(g[:, h * D : (h + 1) * D])
        for j in range(6):
            row = lw[h, 10 + j : 11 + j, :] * level_scale(10 + j)
            g6[h, j * D : (j + 1) * D, :] = (g_t * row).astype(BF16)
    rows = jnp.concatenate([xa[y] for y in range(NY)], 1)
    for c in range(3):
        copies[c].wait()
        part[c] = dot(rows, w_mine[c].reshape(NY * 256, 256))
    for copy in copies[3:]:
        copy.wait()


def project_kernel(xb, w_rest, part, g6, qkv, msg):
    rows = jnp.concatenate([xb[y] for y in range(NY)], 1)
    for c in range(3):
        total = part[c] + dot(rows, w_rest[c].reshape(NY * 256, 256))
        qkv[c] = total.astype(BF16)
    for h in range(H):
        cols = slice(h * D, (h + 1) * D)
        k_t = flipped(qkv[1, :, cols]).astype(BF16)
        state = dot(k_t, qkv[2, :, cols]).astype(BF16)
        grads = dot(g6[h], qkv[0, :, cols]).astype(BF16)
        mats = [state] + [grads[j * D : (j + 1) * D] for j in range(6)]
        for m, mat in enumerate(mats):
            at = m * HQ + h * Q
            for to in range(NG):
                msg[to, at : at + Q, :] = mat[to * Q : (to + 1) * Q]


def spread_kernel(pos, recv, far, low, mats):
    z = pos[1]

    def total(m, sources):
        terms = [recv[s, m * HQ : (m + 1) * HQ, :].astype(F32) for s in sources]
        return sum(terms[1:], terms[0])

    mats[0] = total(0, range(NG)).astype(BF16)
    for m in range(3):
        mats[1 + m] = total(4 + m, range(NG)).astype(BF16)
    for to in range(NZ):
        d = z ^ to
        top = (d >= 2).astype(jnp.int32) + (d >= 4).astype(jnp.int32)
        far[to] = mats[jnp.where(to > z, 0, 1 + top)]
    for j in range(3):
        for first in range(0, NG, 2**j):
            sent = total(1 + j if (first >> j) & 1 else 0, range(first, first + 2**j))
            for to in range(first ^ 2**j, (first ^ 2**j) + 2**j):
                low[to, j * HQ : (j + 1) * HQ, :] = sent.astype(BF16)


def collect_kernel(pos, recv, low, out):
    z = pos[1]
    out[:, : 3 * HQ, :] = low[...]
    for j in range(3):
        first = lax.shift_left(lax.shift_right_logical(z, j) ^ 1, j)
        total = recv[first].astype(F32)
        for i in range(1, 2**j):
            total = total + recv[first + i].astype(F32)
        total = total.astype(BF16)
        for to in range(NG):
            out[to, (j + 3) * HQ : (j + 4) * HQ, :] = total


def attend_kernel(qkv, g_in, lw, out_t, dq_t, dk, dv, a_t, b_t):
    n = T // D
    s_at = lax.broadcasted_iota(jnp.int32, (D, D), 0)
    t_at = lax.broadcasted_iota(jnp.int32, (D, D), 1)
    differ = s_at ^ t_at
    for h in range(H):
        cols = slice(h * D, (h + 1) * D)
        q, k, v, g = qkv[0, :, cols], qkv[1, :, cols], qkv[2, :, cols], g_in[:, cols]
        q_t, k_t, v_t, g_t = (flipped(a).astype(BF16) for a in (q, k, v, g))
        rows = [lw[h, l : l + 1, :] * level_scale(l) for l in range(10)]
        for si in range(n):
            s = slice(si * D, (si + 1) * D)
            scores = dot(k[s], q_t[:, si * D :])
            back = dot(v[s], g_t[:, si * D :])
            for ti in range(si, n):
                t = slice(ti * D, (ti + 1) * D)
                part = slice((ti - si) * D, (ti - si + 1) * D)
                if ti == si:
                    mask = jnp.broadcast_to(rows[0][:, t], (D, D))
                    for l in range(1, 8):
                        mask = jnp.where(differ >= 2 ** (l - 1), rows[l][:, t], mask)
                    mask = jnp.where(t_at >= s_at, mask, 0.0)
                else:
                    mask = rows[8 if ti ^ si == 1 else 9][:, t]
                a_t[s, t] = (scores[:, part] * mask).astype(BF16)
                b_t[s, t] = (back[:, part] * mask).astype(BF16)
            dv[s, cols] = dot(a_t[s, si * D :], g[si * D :]).astype(BF16)
            dk[s, cols] = dot(b_t[s, si * D :], q[si * D :]).astype(BF16)
        for ti in range(n):
            t = slice(ti * D, (ti + 1) * D)
            seen = (ti + 1) * D
            out_t[h, :, t] = dot(v_t[:, :seen], a_t[:seen, t]).astype(BF16)
            dq_t[h, :, t] = dot(k_t[:, :seen], b_t[:seen, t]).astype(BF16)


def finish_kernel(pos, qkv, g_in, lw, recv_c, out_p, dq_p, dk_p, dv_p, out, dq, dk, dv):
    n = pos[2]
    for h in range(H):
        cols = slice(h * D, (h + 1) * D)
        slots = []
        for j in range(6):
            at = j * HQ + h * Q
            slots.append(
                jnp.concatenate([recv_c[src, at : at + Q, :].astype(F32) for src in range(NG)], 0)
            )
        q_t, g_t = flipped(qkv[0, :, cols]), flipped(g_in[:, cols])
        later = jnp.zeros((D, D), F32)
        reads_o, reads_q = [], []
        for j in range(6):
            flag = (lax.shift_right_logical(n, j) & 1).astype(F32)
            row = lw[h, 10 + j : 11 + j, :] * (level_scale(10 + j) * flag)
            reads_o.append((q_t * row).astype(BF16))
            reads_q.append((g_t * row).astype(BF16))
            later = later + slots[j] * (1.0 - flag)
        states = jnp.concatenate(slots, 1).astype(BF16)
        states_t = jnp.concatenate([s.T for s in slots], 1).astype(BF16)
        total_o = out_p[h].astype(F32) + dot(states_t, jnp.concatenate(reads_o, 0))
        total_q = dq_p[h].astype(F32) + dot(states, jnp.concatenate(reads_q, 0))
        later = later.astype(BF16)
        out[:, cols] = total_o.T.astype(BF16)
        dq[:, cols] = total_q.T.astype(BF16)
        dk[:, cols] = (dk_p[:, cols] + dot(qkv[2, :, cols], later)).astype(BF16)
        dv[:, cols] = (dv_p[:, cols] + dot_nt(qkv[1, :, cols], later)).astype(BF16)


SMEM = pl.BlockSpec(memory_space=pltpu.SMEM)
VMEM = pl.BlockSpec(memory_space=pltpu.VMEM)
LEFT = pl.BlockSpec(memory_space=pltpu.HBM)


def call(kernel, pos, args, outs, scratch=(), mib=8, flops=0, left=()):
    shapes = tuple(jax.ShapeDtypeStruct(s, d) for s, d in outs)
    head = () if pos is None else (pos,)
    moved = sum(a.size * a.dtype.itemsize for a in (*args, *shapes))
    return pl.pallas_call(
        kernel,
        out_shape=shapes,
        in_specs=[SMEM] * len(head) + [LEFT if i in left else VMEM for i in range(len(args))],
        out_specs=tuple(VMEM for _ in shapes),
        scratch_shapes=list(scratch),
        cost_estimate=pl.CostEstimate(flops=flops, bytes_accessed=moved, transcendentals=0),
        compiler_params=pltpu.CompilerParams(vmem_limit_bytes=mib * 2**20),
    )(*head, *args)


def swap(value, axis):
    return lax.all_to_all(value, axis, 0, 0, tiled=True)


def body(activations, w_proj, level_weight, g):
    zh, zl, x, core = (lax.axis_index(a) for a in ("zh", "zl", "x", "core"))
    pos = jnp.stack([core, zh, (zh * NL + zl) * NX + x]).astype(jnp.int32)
    lw = jnp.transpose(level_weight, (1, 2, 0))
    w = w_proj.reshape(3, NY, 2, 256, 256)
    half_flops = T * 1024 * 768 * 2
    xa = swap(jnp.broadcast_to(activations[None], (NY, *activations.shape)), "y")
    xb = lax.ppermute(xa, "core", [(0, 1), (1, 0)])
    part, w_rest, g6 = call(
        half_kernel,
        pos,
        (xa, w, lw, g),
        (((3, T, H * D), F32), ((3, NY, 256, 256), BF16), ((H, 6 * D, T), BF16)),
        [pltpu.VMEM((3, NY, 256, 256), BF16), pltpu.SemaphoreType.DMA((2, 3))],
        mib=47,
        flops=half_flops,
        left=(1,),
    )
    qkv, msg = call(
        project_kernel,
        None,
        (xb, w_rest, part, g6),
        (((3, T, H * D), BF16), ((NG, 7 * HQ, D), BF16)),
        flops=half_flops,
    )
    recv_a = swap(msg, ("zl", "x"))
    far, low = call(
        spread_kernel,
        pos,
        (recv_a,),
        (((NZ, HQ, D), BF16), ((NG, 3 * HQ, D), BF16)),
        [pltpu.VMEM((4, HQ, D), BF16)],
    )
    recv_b = swap(far, "zh")
    (back,) = call(collect_kernel, pos, (recv_b, low), (((NG, 6 * HQ, D), BF16),))
    recv_c = swap(back, ("zl", "x"))
    flat, tall = ((T, H * D), BF16), ((H, D, T), BF16)
    parts = call(
        attend_kernel,
        None,
        (qkv, g, lw),
        (tall, tall, flat, flat),
        [pltpu.VMEM((T, T), BF16), pltpu.VMEM((T, T), BF16)],
        flops=2 * H * 6 * T * T * D,
    )
    return call(finish_kernel, pos, (qkv, g, lw, recv_c, *parts), (((T, H * D), BF16),) * 4)


def solution(mesh):
    fine = Mesh(mesh.devices.reshape(NZ, NL, NX, NY, 2), ("zh", "zl", "x", "y", "core"))
    rows, cols = ("zh", "zl", "x"), ("y", "core")
    in_specs = (P(rows, cols), P(None, None, cols), P(rows, cols, None), P(rows, cols))
    return jax.shard_map(
        body, mesh=fine, in_specs=in_specs, out_specs=(P(rows, cols),) * 4, check_vma=False
    )
```

```python
import jax
import jax.numpy as jnp
from jax import lax
from jax.experimental import pallas as pl
from jax.experimental.pallas import tpu as pltpu
from jax.sharding import Mesh, PartitionSpec as P

T = 512
D = 128
H = 2
NX = 4
NL = 2
NG = NX * NL
NZ = 8
NY = 4
FIRST_Y, FIRST_P, FIRST_Z, FIRST_B = 2, 2, 4, 2
Q = D // NG
HQ = H * Q
F32 = jnp.float32
BF16 = jnp.bfloat16


def dot(a, b):
    return jnp.dot(a, b, preferred_element_type=F32)


def dot_nt(a, b):
    return lax.dot_general(a, b, (((1,), (1,)), ((), ())), preferred_element_type=F32)


def flipped(a):
    return a.astype(F32).T


def level_scale(level):
    return 2.0 ** (-(max(level, 1) - 1) / 2) * D**-0.5


def half_kernel(pos, xa, w, lw, g, part, w_rest, g6, w_mine, sems):
    core = pos[0]
    copies = [
        pltpu.make_async_copy(w.at[c, :, side], to.at[c], sems.at[i, c])
        for i, (side, to) in enumerate(((core, w_mine), (1 - core, w_rest)))
        for c in range(3)
    ]
    for copy in copies:
        copy.start()
    for h in range(H):
        g_t = flipped(g[:, h * D : (h + 1) * D])
        for j in range(6):
            row = lw[h, 10 + j : 11 + j, :] * level_scale(10 + j)
            g6[h, j * D : (j + 1) * D, :] = (g_t * row).astype(BF16)
    rows = jnp.concatenate([xa[y ^ FIRST_Y] for y in range(NY)], 1)
    for c in range(3):
        copies[c].wait()
        part[c] = dot(rows, w_mine[c].reshape(NY * 256, 256))
    for copy in copies[3:]:
        copy.wait()


def project_kernel(xb, w_rest, part, g6, qkv, msg):
    rows = jnp.concatenate([xb[y ^ FIRST_Y] for y in range(NY)], 1)
    for c in range(3):
        total = part[c] + dot(rows, w_rest[c].reshape(NY * 256, 256))
        qkv[c] = total.astype(BF16)
    for h in range(H):
        cols = slice(h * D, (h + 1) * D)
        k_t = flipped(qkv[1, :, cols]).astype(BF16)
        state = dot(k_t, qkv[2, :, cols]).astype(BF16)
        grads = dot(g6[h], qkv[0, :, cols]).astype(BF16)
        mats = [state] + [grads[j * D : (j + 1) * D] for j in range(6)]
        for m, mat in enumerate(mats):
            at = m * HQ + h * Q
            for to in range(NG):
                msg[to ^ FIRST_P, at : at + Q, :] = mat[to * Q : (to + 1) * Q]


def spread_kernel(pos, recv, far, low, mats):
    z = pos[1]

    def total(m, sources):
        terms = [recv[s ^ FIRST_P, m * HQ : (m + 1) * HQ, :].astype(F32) for s in sources]
        return sum(terms[1:], terms[0])

    mats[0] = total(0, range(NG)).astype(BF16)
    for m in range(3):
        mats[1 + m] = total(4 + m, range(NG)).astype(BF16)
    for to in range(NZ):
        d = z ^ to
        top = (d >= 2).astype(jnp.int32) + (d >= 4).astype(jnp.int32)
        far[to ^ FIRST_Z] = mats[jnp.where(to > z, 0, 1 + top)]
    for j in range(3):
        for first in range(0, NG, 2**j):
            sent = total(1 + j if (first >> j) & 1 else 0, range(first, first + 2**j))
            for to in range(first ^ 2**j, (first ^ 2**j) + 2**j):
                low[to ^ FIRST_B, j * HQ : (j + 1) * HQ, :] = sent.astype(BF16)


def collect_kernel(pos, recv, low, out):
    z = pos[1]
    out[:, : 3 * HQ, :] = low[...]
    for j in range(3):
        first = lax.shift_left(lax.shift_right_logical(z ^ FIRST_Z, j) ^ 1, j)
        total = recv[first].astype(F32)
        for i in range(1, 2**j):
            total = total + recv[first + i].astype(F32)
        total = total.astype(BF16)
        for to in range(NG):
            out[to, (j + 3) * HQ : (j + 4) * HQ, :] = total


def attend_kernel(qkv, g_in, lw, out_t, dq_t, dk, dv, a_t, b_t):
    n = T // D
    s_at = lax.broadcasted_iota(jnp.int32, (D, D), 0)
    t_at = lax.broadcasted_iota(jnp.int32, (D, D), 1)
    differ = s_at ^ t_at
    for h in range(H):
        cols = slice(h * D, (h + 1) * D)
        q, k, v, g = qkv[0, :, cols], qkv[1, :, cols], qkv[2, :, cols], g_in[:, cols]
        q_t, k_t, v_t, g_t = (flipped(a).astype(BF16) for a in (q, k, v, g))
        rows = [lw[h, l : l + 1, :] * level_scale(l) for l in range(10)]
        for si in range(n):
            s = slice(si * D, (si + 1) * D)
            scores = dot(k[s], q_t[:, si * D :])
            back = dot(v[s], g_t[:, si * D :])
            for ti in range(si, n):
                t = slice(ti * D, (ti + 1) * D)
                part = slice((ti - si) * D, (ti - si + 1) * D)
                if ti == si:
                    mask = jnp.broadcast_to(rows[0][:, t], (D, D))
                    for l in range(1, 8):
                        mask = jnp.where(differ >= 2 ** (l - 1), rows[l][:, t], mask)
                    mask = jnp.where(t_at >= s_at, mask, 0.0)
                else:
                    mask = rows[8 if ti ^ si == 1 else 9][:, t]
                a_t[s, t] = (scores[:, part] * mask).astype(BF16)
                b_t[s, t] = (back[:, part] * mask).astype(BF16)
            dv[s, cols] = dot(a_t[s, si * D :], g[si * D :]).astype(BF16)
            dk[s, cols] = dot(b_t[s, si * D :], q[si * D :]).astype(BF16)
        for ti in range(n):
            t = slice(ti * D, (ti + 1) * D)
            seen = (ti + 1) * D
            out_t[h, :, t] = dot(v_t[:, :seen], a_t[:seen, t]).astype(BF16)
            dq_t[h, :, t] = dot(k_t[:, :seen], b_t[:seen, t]).astype(BF16)


def finish_kernel(pos, qkv, g_in, lw, recv_c, out_p, dq_p, dk_p, dv_p, out, dq, dk, dv):
    n = pos[2]
    for h in range(H):
        cols = slice(h * D, (h + 1) * D)
        slots = []
        for j in range(6):
            at = j * HQ + h * Q
            slots.append(
                jnp.concatenate([recv_c[src ^ FIRST_B, at : at + Q, :].astype(F32) for src in range(NG)], 0)
            )
        q_t, g_t = flipped(qkv[0, :, cols]), flipped(g_in[:, cols])
        later = jnp.zeros((D, D), F32)
        reads_o, reads_q = [], []
        for j in range(6):
            flag = (lax.shift_right_logical(n, j) & 1).astype(F32)
            row = lw[h, 10 + j : 11 + j, :] * (level_scale(10 + j) * flag)
            reads_o.append((q_t * row).astype(BF16))
            reads_q.append((g_t * row).astype(BF16))
            later = later + slots[j] * (1.0 - flag)
        states = jnp.concatenate(slots, 1).astype(BF16)
        states_t = jnp.concatenate([s.T for s in slots], 1).astype(BF16)
        total_o = out_p[h].astype(F32) + dot(states_t, jnp.concatenate(reads_o, 0))
        total_q = dq_p[h].astype(F32) + dot(states, jnp.concatenate(reads_q, 0))
        later = later.astype(BF16)
        out[:, cols] = total_o.T.astype(BF16)
        dq[:, cols] = total_q.T.astype(BF16)
        dk[:, cols] = (dk_p[:, cols] + dot(qkv[2, :, cols], later)).astype(BF16)
        dv[:, cols] = (dv_p[:, cols] + dot_nt(qkv[1, :, cols], later)).astype(BF16)


SMEM = pl.BlockSpec(memory_space=pltpu.SMEM)
VMEM = pl.BlockSpec(memory_space=pltpu.VMEM)
LEFT = pl.BlockSpec(memory_space=pltpu.HBM)


def call(kernel, pos, args, outs, scratch=(), mib=8, flops=0, left=()):
    shapes = tuple(jax.ShapeDtypeStruct(s, d) for s, d in outs)
    head = () if pos is None else (pos,)
    moved = sum(a.size * a.dtype.itemsize for a in (*args, *shapes))
    return pl.pallas_call(
        kernel,
        out_shape=shapes,
        in_specs=[SMEM] * len(head) + [LEFT if i in left else VMEM for i in range(len(args))],
        out_specs=tuple(VMEM for _ in shapes),
        scratch_shapes=list(scratch),
        cost_estimate=pl.CostEstimate(flops=flops, bytes_accessed=moved, transcendentals=0),
        compiler_params=pltpu.CompilerParams(vmem_limit_bytes=mib * 2**20),
    )(*head, *args)


def swap(value, axis, first):
    return lax.all_to_all(value, axis, 0, 0, axis_index_groups=[[i ^ first for i in range(value.shape[0])]], tiled=True)


def body(activations, w_proj, level_weight, g):
    zh, zl, x, core = (lax.axis_index(a) for a in ("zh", "zl", "x", "core"))
    pos = jnp.stack([core, zh, (zh * NL + zl) * NX + x]).astype(jnp.int32)
    lw = jnp.transpose(level_weight, (1, 2, 0))
    w = w_proj.reshape(3, NY, 2, 256, 256)
    half_flops = T * 1024 * 768 * 2
    xa = swap(jnp.broadcast_to(activations[None], (NY, *activations.shape)), "y", FIRST_Y)
    xb = lax.ppermute(xa, "core", [(0, 1), (1, 0)])
    part, w_rest, g6 = call(
        half_kernel,
        pos,
        (xa, w, lw, g),
        (((3, T, H * D), F32), ((3, NY, 256, 256), BF16), ((H, 6 * D, T), BF16)),
        [pltpu.VMEM((3, NY, 256, 256), BF16), pltpu.SemaphoreType.DMA((2, 3))],
        mib=47,
        flops=half_flops,
        left=(1,),
    )
    qkv, msg = call(
        project_kernel,
        None,
        (xb, w_rest, part, g6),
        (((3, T, H * D), BF16), ((NG, 7 * HQ, D), BF16)),
        flops=half_flops,
    )
    recv_a = swap(msg, ("zl", "x"), FIRST_P)
    far, low = call(
        spread_kernel,
        pos,
        (recv_a,),
        (((NZ, HQ, D), BF16), ((NG, 3 * HQ, D), BF16)),
        [pltpu.VMEM((4, HQ, D), BF16)],
    )
    recv_b = swap(far, "zh", FIRST_Z)
    (back,) = call(collect_kernel, pos, (recv_b, low), (((NG, 6 * HQ, D), BF16),))
    recv_c = swap(back, ("zl", "x"), FIRST_B)
    flat, tall = ((T, H * D), BF16), ((H, D, T), BF16)
    parts = call(
        attend_kernel,
        None,
        (qkv, g, lw),
        (tall, tall, flat, flat),
        [pltpu.VMEM((T, T), BF16), pltpu.VMEM((T, T), BF16)],
        flops=2 * H * 6 * T * T * D,
    )
    return call(finish_kernel, pos, (qkv, g, lw, recv_c, *parts), (((T, H * D), BF16),) * 4)


def solution(mesh):
    fine = Mesh(mesh.devices.reshape(NZ, NL, NX, NY, 2), ("zh", "zl", "x", "y", "core"))
    rows, cols = ("zh", "zl", "x"), ("y", "core")
    in_specs = (P(rows, cols), P(None, None, cols), P(rows, cols, None), P(rows, cols))
    return jax.shard_map(
        body, mesh=fine, in_specs=in_specs, out_specs=(P(rows, cols),) * 4, check_vma=False
    )
```

```python
import jax
import jax.numpy as jnp
from jax import lax
from jax.experimental import pallas as pl
from jax.experimental.pallas import tpu as pltpu
from jax.sharding import Mesh, PartitionSpec as P

T = 512
D = 128
H = 2
NX = 4
NL = 2
NG = NX * NL
NZ = 8
NY = 4
FIRST_Y, FIRST_P, FIRST_Z, FIRST_B = 2, 2, 4, 2
Q = D // NG
HQ = H * Q
F32 = jnp.float32
BF16 = jnp.bfloat16


def dot(a, b):
    return jnp.dot(a, b, preferred_element_type=F32)


def dot_nt(a, b):
    return lax.dot_general(a, b, (((1,), (1,)), ((), ())), preferred_element_type=F32)


def flipped(a):
    return a.astype(F32).T


def block_number():
    return (lax.axis_index("zh") * NL + lax.axis_index("zl")) * NX + lax.axis_index("x")


def level_scale(level):
    return 2.0 ** (-(max(level, 1) - 1) / 2) * D**-0.5


def half_kernel(xa, w, lw, g, part, w_rest, g6, w_mine, sems):
    core = lax.axis_index("core")
    mine, rest = (
        [
            pltpu.make_async_copy(w.at[c, :, side], to.at[c], sems.at[i, c])
            for c in range(3)
        ]
        for i, (side, to) in enumerate(((core, w_mine), (1 - core, w_rest)))
    )
    for copy in mine + rest:
        copy.start()
    for h in range(H):
        g_t = flipped(g[:, h * D : (h + 1) * D])
        for j in range(6):
            row = lw[h, 10 + j : 11 + j, :] * level_scale(10 + j)
            g6[h, j * D : (j + 1) * D, :] = (g_t * row).astype(BF16)
    for copy in mine:
        copy.wait()
    rows = jnp.concatenate([xa[y ^ FIRST_Y] for y in range(NY)], 1)
    for c in range(3):
        part[c] = dot(rows, w_mine[c].reshape(NY * 256, 256))
    for copy in rest:
        copy.wait()


def project_kernel(xb, w_rest, part, g6, q_out, k_out, v_out, msg):
    rows = jnp.concatenate([xb[y ^ FIRST_Y] for y in range(NY)], 1)
    outs = []
    for c, ref in enumerate((q_out, k_out, v_out)):
        total = part[c] + dot(rows, w_rest[c].reshape(NY * 256, 256))
        outs.append(total.astype(BF16))
        ref[...] = outs[c]
    q, k, v = outs
    states = dot(flipped(k).astype(BF16), v).astype(BF16)
    grads = [[], []]
    for at in range(0, 6 * D, 256):
        for h in range(H):
            grads[h].append(dot(g6[h, at : at + 256], q)[:, h * D : (h + 1) * D].astype(BF16))
    bits = [(lax.shift_right_logical(block_number(), j) & 1) == 1 for j in range(6)]
    for h in range(H):
        cols = slice(h * D, (h + 1) * D)
        own = jnp.concatenate(grads[h], 0)
        for j in range(6):
            at = j * HQ + h * Q
            mat = jnp.where(bits[j], own[j * D : (j + 1) * D], states[cols, cols])
            for to in range(NG):
                msg[to ^ FIRST_P, at : at + Q, :] = mat[to * Q : (to + 1) * Q]


def spread_kernel(recv, far, low, mats):
    z = lax.axis_index("zh")

    def total(m, sources):
        terms = [recv[s ^ FIRST_P, m * HQ : (m + 1) * HQ, :].astype(F32) for s in sources]
        return sum(terms[1:], terms[0])

    for m in range(3):
        mats[m] = total(3 + m, range(NG)).astype(BF16)
    for to in range(NZ):
        d = z ^ to
        top = (d >= 2).astype(jnp.int32) + (d >= 4).astype(jnp.int32)
        far[to ^ FIRST_Z] = mats[top]
    for j in range(3):
        for first in range(0, NG, 2**j):
            sent = total(j, range(first, first + 2**j)).astype(BF16)
            for to in range(first ^ 2**j, (first ^ 2**j) + 2**j):
                low[to ^ FIRST_B, j * HQ : (j + 1) * HQ, :] = sent


def collect_kernel(recv, low, out):
    z = lax.axis_index("zh")
    out[:, : 3 * HQ, :] = low[...]
    for j in range(3):
        first = lax.shift_left(lax.shift_right_logical(z ^ FIRST_Z, j) ^ 1, j)
        total = recv[first].astype(F32)
        for i in range(1, 2**j):
            total = total + recv[first + i].astype(F32)
        total = total.astype(BF16)
        for to in range(NG):
            out[to, (j + 3) * HQ : (j + 4) * HQ, :] = total


def attend_kernel(q_in, k_in, v_in, g_in, lw, out_t, dq_t, dk, dv, q_flip, g_flip, a_t, b_t):
    n = T // D
    s_at = lax.broadcasted_iota(jnp.int32, (D, D), 0)
    t_at = lax.broadcasted_iota(jnp.int32, (D, D), 1)
    differ = s_at ^ t_at
    for h in range(H):
        cols = slice(h * D, (h + 1) * D)
        q, k, v, g = q_in[:, cols], k_in[:, cols], v_in[:, cols], g_in[:, cols]
        q_t, k_t, v_t, g_t = (flipped(a).astype(BF16) for a in (q, k, v, g))
        q_flip[h] = q_t
        g_flip[h] = g_t
        rows = [lw[h, l : l + 1, :] * level_scale(l) for l in range(10)]
        for si in range(n):
            s = slice(si * D, (si + 1) * D)
            scores = dot(k[s], q_t[:, si * D :])
            back = dot(v[s], g_t[:, si * D :])
            for ti in range(si, n):
                t = slice(ti * D, (ti + 1) * D)
                part = slice((ti - si) * D, (ti - si + 1) * D)
                if ti == si:
                    mask = jnp.broadcast_to(rows[0][:, t], (D, D))
                    for l in range(1, 8):
                        mask = jnp.where(differ >= 2 ** (l - 1), rows[l][:, t], mask)
                    mask = jnp.where(t_at >= s_at, mask, 0.0)
                else:
                    mask = rows[8 if ti ^ si == 1 else 9][:, t]
                a_t[s, t] = (scores[:, part] * mask).astype(BF16)
                b_t[s, t] = (back[:, part] * mask).astype(BF16)
            dv[s, cols] = dot(a_t[s, si * D :], g[si * D :]).astype(BF16)
            dk[s, cols] = dot(b_t[s, si * D :], q[si * D :]).astype(BF16)
        for ti in range(n):
            t = slice(ti * D, (ti + 1) * D)
            seen = (ti + 1) * D
            out_t[h, :, t] = dot(v_t[:, :seen], a_t[:seen, t]).astype(BF16)
            dq_t[h, :, t] = dot(k_t[:, :seen], b_t[:seen, t]).astype(BF16)


def finish_kernel(
    k, v, q_t, g_t, lw, recv, out_p, dq_p, dk_p, dv_p, out, dq, dk, dv, o_buf, dq_buf, dk_buf, dv_buf, sems
):
    n = block_number()
    flags = [(lax.shift_right_logical(n, j) & 1).astype(F32) for j in range(6)]
    slots, later = [], []
    for h in range(H):
        slots.append([])
        for j in range(6):
            at = j * HQ + h * Q
            slots[h].append(
                jnp.concatenate([recv[src ^ FIRST_B, at : at + Q, :] for src in range(NG)], 0)
            )
        later.append(sum(m.astype(F32) * (1.0 - f) for m, f in zip(slots[h], flags)).astype(BF16))
    none = jnp.zeros((D, D), BF16)
    both = jnp.concatenate(
        [jnp.concatenate([later[0], none], 1), jnp.concatenate([none, later[1]], 1)], 0
    )
    copies = []

    def send(buf, to, cols, i):
        copies.append(pltpu.make_async_copy(buf.at[:, cols], to.at[:, cols], sems.at[i]))
        copies[-1].start()

    for h in range(H):
        cols = slice(h * D, (h + 1) * D)
        rows = [
            (lw[h, 10 + j : 11 + j, :] * (level_scale(10 + j) * flags[j])).astype(BF16)
            for j in range(6)
        ]
        states_t = jnp.concatenate([flipped(m).astype(BF16) for m in slots[h]], 1)
        reads = jnp.concatenate([q_t[h] * row for row in rows], 0)
        o_buf[:, cols] = (out_p[h] + dot(states_t, reads)).T.astype(BF16)
        send(o_buf, out, cols, 2 + h)
        states = jnp.concatenate(slots[h], 1)
        reads = jnp.concatenate([g_t[h] * row for row in rows], 0)
        dq_buf[:, cols] = (dq_p[h] + dot(states, reads)).T.astype(BF16)
        send(dq_buf, dq, cols, 4 + h)
    dk_buf[...] = (dk_p[...] + dot(v[...], both)).astype(BF16)
    send(dk_buf, dk, slice(0, H * D), 0)
    dv_buf[...] = (dv_p[...] + dot_nt(k[...], both)).astype(BF16)
    send(dv_buf, dv, slice(0, H * D), 1)
    for copy in copies:
        copy.wait()


VMEM = pl.BlockSpec(memory_space=pltpu.VMEM)
LEFT = pl.BlockSpec(memory_space=pltpu.HBM)


def call(kernel, args, outs, scratch=(), mib=8, flops=0, left=(), away=False):
    shapes = tuple(jax.ShapeDtypeStruct(s, d) for s, d in outs)
    moved = sum(a.size * a.dtype.itemsize for a in (*args, *shapes))
    return pl.pallas_call(
        kernel,
        out_shape=shapes,
        in_specs=[LEFT if i in left else VMEM for i in range(len(args))],
        out_specs=tuple(LEFT if away else VMEM for _ in shapes),
        scratch_shapes=list(scratch),
        cost_estimate=pl.CostEstimate(flops=flops, bytes_accessed=moved, transcendentals=0),
        compiler_params=pltpu.CompilerParams(vmem_limit_bytes=mib * 2**20),
    )(*args)


def swap(value, axis, first):
    return lax.all_to_all(value, axis, 0, 0, axis_index_groups=[[i ^ first for i in range(value.shape[0])]], tiled=True)


def body(activations, w_proj, level_weight, g):
    lw = jnp.transpose(level_weight, (1, 2, 0))
    w = w_proj.reshape(3, NY, 2, 256, 256)
    tokens = ((T, H * D), BF16)
    half_flops = T * 1024 * 768 * 2
    xa = swap(jnp.broadcast_to(activations[None], (NY, *activations.shape)), "y", FIRST_Y)
    xb = lax.ppermute(xa, "core", [(0, 1), (1, 0)])
    part, w_rest, g6 = call(
        half_kernel,
        (xa, w, lw, g),
        (((3, T, H * D), F32), ((3, NY, 256, 256), BF16), ((H, 6 * D, T), BF16)),
        [pltpu.VMEM((3, NY, 256, 256), BF16), pltpu.SemaphoreType.DMA((2, 3))],
        mib=47,
        flops=half_flops,
        left=(1,),
    )
    q, k, v, msg = call(
        project_kernel,
        (xb, w_rest, part, g6),
        (tokens, tokens, tokens, ((NG, 6 * HQ, D), BF16)),
        flops=half_flops,
    )
    recv_a = swap(msg, ("zl", "x"), FIRST_P)
    far, low = call(
        spread_kernel,
        (recv_a,),
        (((NZ, HQ, D), BF16), ((NG, 3 * HQ, D), BF16)),
        [pltpu.VMEM((3, HQ, D), BF16)],
    )
    recv_b = swap(far, "zh", FIRST_Z)
    (back,) = call(collect_kernel, (recv_b, low), (((NG, 6 * HQ, D), BF16),))
    recv_c = swap(back, ("zl", "x"), FIRST_B)
    tall = ((H, D, T), BF16)
    *parts, q_t, g_t = call(
        attend_kernel,
        (q, k, v, g, lw),
        (tall, tall, tokens, tokens, tall, tall),
        [pltpu.VMEM((T, T), BF16), pltpu.VMEM((T, T), BF16)],
        flops=2 * H * 6 * T * T * D,
    )
    return call(
        finish_kernel,
        (k, v, q_t, g_t, lw, recv_c, *parts),
        (tokens,) * 4,
        [pltpu.VMEM((T, H * D), BF16)] * 4 + [pltpu.SemaphoreType.DMA((6,))],
        away=True,
    )


def solution(mesh):
    fine = Mesh(mesh.devices.reshape(NZ, NL, NX, NY, 2), ("zh", "zl", "x", "y", "core"))
    rows, cols = ("zh", "zl", "x"), ("y", "core")
    in_specs = (P(rows, cols), P(None, None, cols), P(rows, cols, None), P(rows, cols))
    return jax.shard_map(
        body, mesh=fine, in_specs=in_specs, out_specs=(P(rows, cols),) * 4, check_vma=False
    )
```
